32 devices in a mesh: seq: 4 (over z), chan: 4 (over y, x), rep: 2 (over core).
Axes of the slice: x: 2, y: 2, z: 4, core: 2. Of those that a mesh axis runs over, the one named last changes fastest.
Arguments:
- fine_codes: int32 [8192], P(('rep', 'seq')), parts along dimension 0, may hold values from 0 to 1023
- coarse_codes: int32 [4096], P(('rep', 'seq')), parts along dimension 0, may hold values from 0 to 1023
- frame_order: int32 [256], replicated, may hold values from 0 to 255, each once
- emb_fine: bfloat16 [1024, 4096], P(None, 'chan'), may hold values from -90 to 90
- emb_coarse: bfloat16 [1024, 4096], P(None, 'chan'), may hold values from -90 to 90
- norm_gain: bfloat16 [4096], P('chan'), may hold values from 0.099609375 to 1.8984375
- w_hyena: bfloat16 [4096, 3, 4096], P(None, None, 'chan'), may hold values from -0.09375 to 0.09375
- short_taps: bfloat16 [3, 256, 128], P(None, 'chan'), may hold values from -0.5 to 0.5
- long_filter: float32 [4096, 4096], P(('chan', 'seq')), may hold values from -5 to 5
- w_attn: bfloat16 [4096, 3, 2048], P(None, None, 'chan'), may hold values from -0.09375 to 0.09375
Outputs:
- hyena_out: bfloat16 [4096, 8192], P('chan', ('rep', 'seq')), parts along dimension 1
- attn_out: bfloat16 [8192, 2048], P(('rep', 'seq'), 'chan'), parts along dimension 0
The draws below stay inside these ranges and needn't reach their ends.
There are 2 independent parts, one for each index of `rep`. The reference program is written for one: setup_inputs(seed, part) draws one part's arguments, and reference() takes and returns one part's arrays. A program takes and returns all parts, laid end to end along the dimension named above; an argument that names none is the same for every part. Nothing has to cross between parts.
Inputs may be any that keep to these rules, and one draw needn't show every extreme that they name: `frame_order`: each of 0 to 255 once.
All inputs are finite; a program needn't handle non-finite values.
Results may differ from the reference program's by a relative error of at most 0.014.
The reference program's roundings to bfloat16 on the way count: a program that leaves them out, or rounds other values in their place, can miss the bound.
Values may be sent and summed in bfloat16 or wider, within the bound.
No kernel may reach another device: no remote copies, remote signals or barrier semaphores. Data moves between devices by JAX's collectives and lax.ppermute only.
A program may use at most 192 MiB of HBM per device.

```python
import math
import jax
import jax.numpy as jnp
import numpy as np
from jax import lax

MODEL_WIDTH = 4096
HEADS = 16
HD = 128
VOCAB = 1024
TAPS = 128
FIR_GROUP = 16
FRAME = 256
BLOCK = 512
WINDOW_LENGTH = 4096


def table_draw(key, stream):
    row_key, column_key, base_key = jax.random.split(jax.random.fold_in(key, stream), 3)
    column_index = jnp.arange(MODEL_WIDTH, dtype=jnp.float32)
    rising = jnp.exp(column_index * (math.log(10.0) / MODEL_WIDTH))[None, :]
    jitter = jnp.exp(jax.random.uniform(column_key, (1, MODEL_WIDTH), jnp.float32, math.log(0.6), math.log(1.6)))
    row_scale = jnp.exp(jax.random.uniform(row_key, (VOCAB, 1), jnp.float32, 0.0, math.log(10.0)))
    entries = jnp.clip(jax.random.normal(base_key, (VOCAB, MODEL_WIDTH), jnp.float32), -5.0, 5.0)
    return entries * row_scale * rising * jitter * 0.1


def draw_emb_fine(key, part):
    return table_draw(key, 3).astype(jnp.bfloat16)


def draw_emb_coarse(key, part):
    return table_draw(key, 5).astype(jnp.bfloat16)


def draw_long_filter(key, part):
    reach_key, noise_key, position_random_key, height_random_key = jax.random.split(jax.random.fold_in(key, 7), 4)
    low_end = math.log(40.0)
    high_end = math.log(2.0 * WINDOW_LENGTH)
    reaches = jnp.exp(jax.random.uniform(reach_key, (MODEL_WIDTH, 1), jnp.float32, low_end, high_end))
    temporal_delay = jnp.arange(WINDOW_LENGTH, dtype=jnp.int32)[None, :]
    decay_profile = jnp.exp(-temporal_delay.astype(jnp.float32) / reaches)
    spike_position = jax.random.randint(position_random_key, (MODEL_WIDTH, 3), 0, WINDOW_LENGTH)
    spike_height = jax.random.uniform(height_random_key, (MODEL_WIDTH, 3), jnp.float32, 0.5, 0.8)
    for spike_index in range(3):
        spike_mask = temporal_delay >= spike_position[:, spike_index:spike_index + 1]
        decay_profile = decay_profile * jnp.where(spike_mask, spike_height[:, spike_index:spike_index + 1], 1.0)
    entries = jnp.clip(jax.random.normal(noise_key, (MODEL_WIDTH, WINDOW_LENGTH), jnp.float32), -5.0, 5.0)
    energy = jnp.sqrt(jnp.sum(decay_profile * decay_profile, axis=1, keepdims=True))
    return entries * decay_profile / energy


def place_ends(array, stream_key, low, largest):
    extent = array.shape
    spot = [jax.random.randint(jax.random.fold_in(stream_key, axis), (), 0, extent[axis]) for axis in range(len(extent))]
    array = array.at[tuple(spot)].set(low)
    longest = extent.index(max(extent))
    spot[longest] = (spot[longest] + 1) % extent[longest]
    return array.at[tuple(spot)].set(largest)


def steps_of(rng, extent, pieces, low, high):
    level = 1.0
    for axis_at, shards_of in pieces:
        steps = jax.random.uniform(jax.random.fold_in(jax.random.fold_in(rng, 6), axis_at), (shards_of,), jnp.float32, low / len(pieces), high / len(pieces))
        level = level * jnp.repeat(jnp.exp(steps), extent[axis_at] // shards_of).reshape((-1,) + (1,) * (len(extent) - 1 - axis_at))
    return level


def rank_table(number_of, skew):
    portions = [(1 << 20) // math.isqrt(rank ** skew) + 1 for rank in range(1, number_of + 1)]
    width = 1 + sum(portions) // (1 << 30)
    return np.cumsum(np.array([max(1, weight // width) for weight in portions]))


def skewed_ids(own_key, shape, number_of, skew):
    grid = rank_table(number_of, skew)
    ticket = jax.random.randint(jax.random.fold_in(own_key, 1), shape, 0, int(grid[number_of - 1]))
    grade = jnp.searchsorted(jnp.asarray(grid, jnp.int32), ticket, side="right")
    return jax.random.permutation(jax.random.fold_in(own_key, 2), number_of)[grade].astype(jnp.int32)


def normal_values(own_key, shape, deviation, reach, shards=(), held_as=jnp.bfloat16):
    drawn = deviation * jax.random.normal(own_key, shape, jnp.float32)
    if shards:
        drawn = drawn * steps_of(own_key, shape, shards, -0.22, 0.18)
    return jnp.clip(drawn, -reach, reach).astype(held_as)


def setup_inputs(seed: int = 0, part: int = 0) -> dict:
    keys = jax.random.split(jax.random.key(seed), 11)
    part_keys = jax.random.split(jax.random.fold_in(keys[10], part), 11)
    return {
        "fine_codes": place_ends(skewed_ids(part_keys[0], (WINDOW_LENGTH,), VOCAB, 2), jax.random.fold_in(part_keys[0], 3), 0, VOCAB - 1).astype(jnp.int32),
        "coarse_codes": place_ends(skewed_ids(part_keys[1], (WINDOW_LENGTH // 2,), VOCAB, 1), jax.random.fold_in(part_keys[1], 3), 0, VOCAB - 1).astype(jnp.int32),
        "frame_order": jax.random.permutation(keys[2], FRAME).astype(jnp.int32),
        "emb_fine": draw_emb_fine(jax.random.fold_in(keys[10], 71), part),
        "emb_coarse": draw_emb_coarse(jax.random.fold_in(keys[10], 71), part),
        "norm_gain": jnp.clip(1.0 + 0.18 * jax.random.normal(keys[5], (MODEL_WIDTH,), jnp.float32), 0.099609375, 1.8984375).astype(jnp.bfloat16),
        "w_hyena": normal_values(keys[6], (MODEL_WIDTH, 3, MODEL_WIDTH), MODEL_WIDTH ** -0.5, 0.09375, ((2, 4),)),
        "short_taps": normal_values(keys[7], (3, MODEL_WIDTH // FIR_GROUP, TAPS), TAPS ** -0.5, 0.5, ((1, 4),)),
        "long_filter": draw_long_filter(jax.random.fold_in(keys[10], 71), part),
        "w_attn": normal_values(keys[9], (MODEL_WIDTH, 3, HEADS * HD), MODEL_WIDTH ** -0.5, 0.09375, ((2, 4),)),
    }


EPSILON = 1e-05

def rounded(tensor):
    return lax.optimization_barrier(tensor.astype(jnp.bfloat16)).astype(jnp.float32)

def banded(filter_taps):
    tap_count = filter_taps.shape[-1]
    row_index = lax.broadcasted_iota(jnp.int32, (tap_count, 2 * tap_count), 0)
    column_index = lax.broadcasted_iota(jnp.int32, (tap_count, 2 * tap_count), 1)
    tap_lag = row_index + tap_count - column_index
    which_tap = lax.broadcasted_iota(jnp.int32, (tap_count, tap_count, 2 * tap_count), 0)
    selector = (which_tap == tap_lag[None]).astype(filter_taps.dtype)
    flat_taps = filter_taps.reshape(-1, tap_count)
    spread_taps = jnp.dot(flat_taps, selector.reshape(tap_count, -1), preferred_element_type=jnp.float32)
    return spread_taps.reshape(filter_taps.shape[:-1] + (tap_count, 2 * tap_count)).astype(filter_taps.dtype)

def short_filter(sequence, filter_taps):
    channels, length = sequence.shape
    groups, tap_count = filter_taps.shape
    tile_count = length // tap_count
    padded = jnp.concatenate([jnp.zeros((channels, tap_count), sequence.dtype), sequence], axis=1)
    earlier_rows = padded[:, :length].reshape(groups, channels // groups, tile_count, tap_count)
    later_rows = padded[:, tap_count:].reshape(groups, channels // groups, tile_count, tap_count)
    window = jnp.concatenate([earlier_rows, later_rows], axis=3)
    toeplitz = banded(filter_taps).astype(jnp.float32)
    output = jnp.einsum('gab,gcnb->gcna', toeplitz, window.astype(jnp.float32), precision=lax.Precision.HIGHEST)
    return output.reshape(channels, length).astype(jnp.bfloat16)

def filter_one(operands):
    return short_filter(operands[0], operands[1])

def reference(fine_codes, coarse_codes, frame_order, emb_fine, emb_coarse, norm_gain, w_hyena, short_taps, long_filter, w_attn):
    peak_value = lax.Precision.HIGHEST
    frame_base = jnp.arange(WINDOW_LENGTH // FRAME, dtype=jnp.int32) * FRAME
    code_at = (frame_base[:, None] + frame_order.astype(jnp.int32)[None, :]).reshape(WINDOW_LENGTH)
    fine_ids = fine_codes[code_at]
    coarse_ids = coarse_codes[code_at // 2]
    values = rounded(emb_fine[fine_ids].astype(jnp.float32) + emb_coarse[coarse_ids].astype(jnp.float32))
    factor = lax.rsqrt(lax.optimization_barrier(jnp.mean(values * values, axis=1)) + EPSILON)
    normed = (values * factor[:, None] * norm_gain.astype(jnp.float32)[None, :]).astype(jnp.bfloat16)
    projected = jnp.dot(normed, w_hyena.reshape(MODEL_WIDTH, 3 * MODEL_WIDTH), preferred_element_type=jnp.float32)
    projected = projected.astype(jnp.bfloat16).reshape(WINDOW_LENGTH, 3, MODEL_WIDTH).transpose(1, 2, 0)
    filtered = lax.optimization_barrier(lax.map(filter_one, (projected, short_taps))).astype(jnp.float32)
    mixture = rounded(filtered[1] * filtered[2])
    spectrum = jnp.fft.rfft(mixture, n=2 * WINDOW_LENGTH, axis=1) * jnp.fft.rfft(long_filter, n=2 * WINDOW_LENGTH, axis=1)
    convolved = rounded(jnp.fft.irfft(spectrum, n=2 * WINDOW_LENGTH, axis=1)[:, :WINDOW_LENGTH])
    hyena_out = (filtered[0] * convolved).astype(jnp.bfloat16)
    blocks = WINDOW_LENGTH // BLOCK
    heads_all = jnp.dot(hyena_out.T, w_attn.reshape(MODEL_WIDTH, 3 * HEADS * HD), preferred_element_type=jnp.float32)
    heads_all = rounded(heads_all).reshape(blocks, BLOCK, 3, HEADS, HD)
    queries = heads_all[:, :, 0]
    keys_all = heads_all[:, :, 1]
    values_all = heads_all[:, :, 2]
    states = jnp.einsum('nshd,nshe->nhde', keys_all, values_all, precision=peak_value)
    running = jnp.cumsum(states, axis=0)
    earlier = rounded(jnp.concatenate([jnp.zeros_like(states[:1]), running[:-1]], axis=0))
    scores = jnp.einsum('nthd,nshd->nhts', queries, keys_all, precision=peak_value)
    causal = lax.broadcasted_iota(jnp.int32, (BLOCK, BLOCK), 0) >= lax.broadcasted_iota(jnp.int32, (BLOCK, BLOCK), 1)
    scores = rounded(jnp.where(causal, scores, 0.0))
    inside = jnp.einsum('nhts,nshe->nthe', scores, values_all, precision=peak_value)
    carried = jnp.einsum('nthd,nhde->nthe', queries, earlier, precision=peak_value)
    position = jnp.arange(WINDOW_LENGTH, dtype=jnp.int32).reshape(blocks, BLOCK) + 1
    divisor = jnp.sqrt((position * HD).astype(jnp.float32))
    attn_out = ((inside + carried) / divisor[:, :, None, None]).astype(jnp.bfloat16).reshape(WINDOW_LENGTH, HEADS * HD)
    return (hyena_out, attn_out)
```

```python
import functools
import math

import jax
import jax.numpy as jnp
import numpy as np
from jax import lax
from jax.experimental import pallas as pl
from jax.experimental.pallas import tpu as pltpu
from jax.sharding import PartitionSpec as P

HD = 128
FRAME = 256
BLOCK = 512
LANES = 128
EPSILON = 1e-05
F32 = jnp.float32
BF16 = jnp.bfloat16
RING = (0, 1, 3, 2)


def params(vmem_mib=40, **kw):
    return pltpu.CompilerParams(vmem_limit_bytes=vmem_mib << 20, **kw)


def struct(shape, dtype):
    return jax.ShapeDtypeStruct(shape, dtype)


def ring_steps():
    forward = [(RING[i], RING[(i + 1) % 4]) for i in range(4)]
    return forward, [(b, a) for a, b in forward]


def gather_piece(piece, axis, clockwise):
    size = lax.axis_size(axis)
    if size == 4:
        forward, backward = ring_steps()
        left = lax.ppermute(piece, axis, forward)
        right = lax.ppermute(piece, axis, backward)
        if clockwise:
            across = lax.ppermute(left, axis, forward)
        else:
            across = lax.ppermute(right, axis, backward)
        return [piece, left, right, across]
    gathered = lax.all_gather(piece, axis)
    return [gathered[i] for i in range(size)]


def slot_owner(size, slot, me):
    if size != 4:
        return slot
    if slot == 0:
        return me
    if slot == 3:
        return 3 - me
    before = jnp.where(me == 0, 2, jnp.where(me == 1, 0, jnp.where(me == 2, 3, 1)))
    return before if slot == 1 else 3 - before


def shifted(piece, axis, by):
    size = lax.axis_size(axis)
    return lax.ppermute(piece, axis, [(i, (i + by) % size) for i in range(size)])


def passed_along(x, axis, by):
    size = lax.axis_size(axis)
    return lax.ppermute(x, axis, [(i, i + by) for i in range(size - by)])


def embed_kernel(order_ref, fine_ref, coarse_ref, fine_table, coarse_table, *outs):
    frames = fine_ref.shape[0]
    vocab = fine_table.shape[0]
    order = order_ref[...]
    pick = (order == lax.broadcasted_iota(jnp.int32, (FRAME, FRAME), 0)).astype(F32).T
    half = order >> 1
    pick_half = (half == lax.broadcasted_iota(jnp.int32, (FRAME // 2, FRAME), 0)).astype(F32).T
    codes = lax.broadcasted_iota(jnp.int32, (FRAME, vocab), 1).astype(F32)
    per_frame = len(outs) // frames
    rows = FRAME // per_frame
    for f in range(frames):
        fine = jnp.sum(pick * fine_ref[f : f + 1, :].astype(F32), axis=1, keepdims=True)
        coarse = jnp.sum(pick_half * coarse_ref[f : f + 1, :].astype(F32), axis=1, keepdims=True)
        hot_fine = (codes == fine).astype(F32).astype(BF16)
        hot_coarse = (codes == coarse).astype(F32).astype(BF16)
        total = jnp.dot(hot_fine, fine_table[...], preferred_element_type=F32) + jnp.dot(
            hot_coarse, coarse_table[...], preferred_element_type=F32
        )
        total = total.astype(BF16)
        for i in range(per_frame):
            outs[f * per_frame + i][...] = total[i * rows : (i + 1) * rows, :]


def embed(order, fine, coarse, fine_table, coarse_table, piece):
    count = fine.size // piece
    width = fine_table.shape[1]
    return pl.pallas_call(
        embed_kernel,
        out_shape=[struct((piece, width), BF16)] * count,
        compiler_params=params(),
        name="embed",
    )(order, fine, coarse, fine_table, coarse_table)


def project_kernel(slots, chunks, me_ref, *refs):
    del me_ref
    pieces = refs[: slots * chunks]
    gains = refs[slots * chunks : slots * (chunks + 1)]
    weights = refs[slots * (chunks + 1) : slots * (chunks + 2)]
    out_ref, normed = refs[slots * (chunks + 2) :]
    width = pieces[0].shape[1]
    rows = pieces[0].shape[0]

    @pl.when((pl.program_id(0) == 0) & (pl.program_id(1) == 0))
    def _():
        for p in range(chunks):
            total = jnp.zeros((rows, 1), F32)
            for s in range(slots):
                v = pieces[p * slots + s][...].astype(F32)
                total = total + jnp.sum(v * v, axis=1, keepdims=True)
            factor = lax.rsqrt(total / (slots * width) + EPSILON)
            for s in range(slots):
                v = pieces[p * slots + s][...].astype(F32)
                v = v * factor * gains[s][...].astype(F32)
                normed[p * rows : (p + 1) * rows, s * width : (s + 1) * width] = v.astype(BF16)

    acc = None
    for s in range(slots):
        part = jnp.dot(
            normed[:, s * width : (s + 1) * width], weights[s][0], preferred_element_type=F32
        )
        acc = part if acc is None else acc + part
    out_ref[0] = acc.T.astype(BF16)


def project(me, groups, gains, weight):
    chunks = len(groups)
    slots = len(groups[0])
    rows, width = groups[0][0].shape
    streams, _, channels = weight.shape
    block = min(256, channels)
    time = rows * chunks
    whole = lambda k, j, me: (0, 0)
    in_specs = [pl.BlockSpec((rows, width), whole)] * (slots * chunks)
    in_specs += [pl.BlockSpec((1, width), whole)] * slots
    for s in range(slots):
        in_specs.append(
            pl.BlockSpec(
                (1, width, block),
                functools.partial(lambda s, k, j, me: (k, slot_owner(slots, s, me[0]), j), s),
            )
        )
    flops = 2 * time * streams * channels * slots * width
    return pl.pallas_call(
        functools.partial(project_kernel, slots, chunks),
        grid_spec=pltpu.PrefetchScalarGridSpec(
            num_scalar_prefetch=1,
            grid=(streams, channels // block),
            in_specs=in_specs,
            out_specs=pl.BlockSpec((1, block, time), lambda k, j, me: (k, j, 0)),
            scratch_shapes=[pltpu.VMEM((time, slots * width), BF16)],
        ),
        out_shape=struct((streams, channels, time), BF16),
        compiler_params=params(dimension_semantics=("arbitrary", "arbitrary")),
        cost_estimate=pl.CostEstimate(
            flops=flops, transcendentals=0, bytes_accessed=2 * weight.size + 8 * time * slots * width
        ),
        name="project",
    )(me, *[x for g in groups for x in g], *gains, *([weight] * slots))


def short_kernel(count, seq, steps, group, me_ref, taps_ref, *refs):
    tiles = refs[: count + 1]
    first_ref = refs[count + 1]
    mixes = refs[count + 2 : count + 2 + seq]
    step = pl.program_id(0)
    block = tiles[0].shape[1]
    groups = block // group
    part = (step // steps + me_ref[0]) % seq
    base = (part * steps + step % steps) * groups
    row = lax.broadcasted_iota(jnp.int32, (LANES, LANES), 0)
    column = lax.broadcasted_iota(jnp.int32, (LANES, LANES), 1)
    lower = column >= row
    results = []
    for g in range(groups):
        span = slice(g * group, (g + 1) * group)
        outs = []
        for k in range(3):
            tap = jnp.broadcast_to(taps_ref[k, pl.ds(base + g, 1), :], (LANES, LANES))
            turned = pltpu.roll(tap, 0, 1, stride=1, stride_axis=0)
            matrix = jnp.concatenate(
                [jnp.where(lower, 0.0, turned), jnp.where(lower, turned, 0.0)], axis=0
            ).astype(BF16)
            data = [t[k, span, :] for t in tiles]
            window = jnp.concatenate(
                [jnp.concatenate([data[n], data[n + 1]], axis=1) for n in range(count)], axis=0
            )
            outs.append(jnp.dot(window, matrix, preferred_element_type=F32).astype(BF16))
        mix = (outs[1].astype(F32) * outs[2].astype(F32)).astype(BF16)
        results.append((span, outs[0], mix))
    for span, first, mix in results:
        for n in range(count):
            first_ref[span, n * LANES : (n + 1) * LANES] = first[n * group : (n + 1) * group]
    for s in range(seq):

        @pl.when(step // steps == s)
        def _():
            for span, first, mix in results:
                for n in range(count):
                    mixes[s][span, n * LANES : (n + 1) * LANES] = mix[n * group : (n + 1) * group]


def short_filter(place, taps, tiles, seq, group):
    count = len(tiles) - 1
    streams, channels, _ = tiles[0][0].shape
    part = channels // seq
    block = min(LANES, part)
    steps = part // block

    def natural(i, me):
        return ((i // steps + me[0]) % seq) * steps + i % steps

    in_specs = [pl.BlockSpec(taps.shape, lambda i, me: (0, 0, 0))]
    for _, tile in tiles:
        in_specs.append(
            pl.BlockSpec(
                (streams, block, LANES),
                functools.partial(lambda tile, i, me: (0, natural(i, me), tile), tile),
            )
        )
    out_specs = [pl.BlockSpec((block, count * LANES), lambda i, me: (natural(i, me), 0))]
    for s in range(seq):
        out_specs.append(
            pl.BlockSpec(
                (block, count * LANES),
                functools.partial(
                    lambda s, i, me: (jnp.clip(i - s * steps, 0, steps - 1), 0), s
                ),
            )
        )
    outs = pl.pallas_call(
        functools.partial(short_kernel, count, seq, steps, group),
        grid_spec=pltpu.PrefetchScalarGridSpec(
            num_scalar_prefetch=1, grid=(seq * steps,), in_specs=in_specs, out_specs=out_specs
        ),
        out_shape=[struct((channels, count * LANES), BF16)]
        + [struct((part, count * LANES), BF16)] * seq,
        compiler_params=params(dimension_semantics=("arbitrary",)),
        cost_estimate=pl.CostEstimate(
            flops=2 * streams * channels * count * LANES * 2 * LANES * 4,
            transcendentals=0,
            bytes_accessed=2 * channels * LANES * (4 * streams + 4 * count),
        ),
        name="short_filter",
    )(place, taps, *[a for a, _ in tiles])
    return outs[0], outs[1:]


def times_root(value, turn):
    re, im = value
    eighths = turn * 8 % 8
    if eighths == 0:
        return re, im
    if eighths == 2:
        return im, -re
    if eighths == 4:
        return -re, -im
    if eighths == 6:
        return -im, re
    if eighths in (1, 3, 5, 7):
        h = math.sqrt(0.5)
        c = h if eighths in (1, 7) else -h
        s = h if eighths in (1, 3) else -h
        if c == s:
            return (re + im) * c, (im - re) * c
        return (re - im) * c, (im + re) * c
    c, s = math.cos(2 * math.pi * turn), math.sin(2 * math.pi * turn)
    return re * c + im * s, im * c - re * s


def fft(values, sign):
    n = len(values)
    if n == 1:
        return values
    even = fft(values[0::2], sign)
    odd = fft(values[1::2], sign)
    low, high = [], []
    for k in range(n // 2):
        er, ei = even[k]
        tr, ti = times_root(odd[k], sign * k / n)
        low.append((er + tr, ei + ti))
        high.append((er - tr, ei - ti))
    return low + high


def split(x):
    high = x.astype(BF16)
    return high, (x - high.astype(F32)).astype(BF16)


def product3(x, high_ref, low_ref):
    high, low = split(x)
    return (
        jnp.dot(high, low_ref[...], preferred_element_type=F32)
        + jnp.dot(low, high_ref[...], preferred_element_type=F32)
        + jnp.dot(high, high_ref[...], preferred_element_type=F32)
    )


def forward_rows(load, twist_ref, work, count):
    def body(r, carry):
        at = pl.ds(pl.multiple_of(r * 8, 8), 8)
        values = []
        for q in range(count):
            x = load(q, at)
            turn = 2 * math.pi * q / (4 * count)
            values.append((x * math.cos(turn), x * -math.sin(turn)) if q else (x, jnp.zeros_like(x)))
        for u, (re, im) in enumerate(fft(values, 1)):
            c = twist_ref[u : u + 1, :LANES]
            s = twist_ref[u : u + 1, LANES:]
            work[u, at, :LANES] = re * c + im * s
            work[u, at, LANES:] = im * c - re * s
        return carry

    lax.fori_loop(0, work.shape[1] // 8, body, 0)


def spectrum_kernel(x_ref, twist_ref, high_ref, low_ref, out_ref, work):
    count, rows, width = work.shape
    forward_rows(lambda q, at: x_ref[at, q * LANES : (q + 1) * LANES], twist_ref, work, count)
    scale = 2.0 / (2 * count * LANES)

    def inner(u, carry):
        x = work[pl.ds(u * 4, 4)].reshape(4 * rows, width)
        out_ref[pl.ds(u * 4, 4)] = (product3(x, high_ref, low_ref) * (scale / 1.0)).reshape(4, rows, width)
        return carry

    lax.fori_loop(0, count // 4, inner, 0)


def tables(count):
    total = 2 * count * LANES
    u = np.arange(count)[:, None]
    k = np.arange(LANES)[None, :]
    angle = 2 * np.pi * (2 * u + 0.5) * k / total
    twist = np.concatenate([np.cos(angle), np.sin(angle)], axis=1).astype(np.float32)
    inner = 2 * np.pi * (np.arange(LANES)[:, None] * k % LANES) / LANES
    c, s = np.cos(inner), np.sin(inner)
    matrix = np.block([[c, -s], [s, c]]).astype(np.float32)
    high = matrix.astype(jnp.bfloat16)
    low = (matrix - high.astype(np.float32)).astype(jnp.bfloat16)
    return (
        jnp.asarray(twist),
        jnp.asarray(high),
        jnp.asarray(low),
        jnp.asarray(high.T.copy()),
        jnp.asarray(low.T.copy()),
    )


def spectrum(response, table, block):
    channels, length = response.shape
    count = length // LANES
    twist, high, low = table[:3]
    const = lambda i: (0, 0)
    return pl.pallas_call(
        spectrum_kernel,
        grid=(channels // block,),
        in_specs=[
            pl.BlockSpec((block, length), lambda i: (i, 0)),
            pl.BlockSpec(twist.shape, const),
            pl.BlockSpec(high.shape, const),
            pl.BlockSpec(low.shape, const),
        ],
        out_specs=pl.BlockSpec((count, block, 2 * LANES), lambda i: (0, i, 0)),
        out_shape=struct((count, channels, 2 * LANES), F32),
        scratch_shapes=[pltpu.VMEM((count, block, 2 * LANES), F32)],
        compiler_params=params(dimension_semantics=("arbitrary",)),
        cost_estimate=pl.CostEstimate(
            flops=channels * count * 2 * 256 * 256 * 6, transcendentals=0, bytes_accessed=12 * channels * length
        ),
        name="spectrum",
    )(response, twist, high, low)


def conv_kernel(layout, seq, me_ref, *refs):
    pieces = refs[: len(layout)]
    spec_ref, twist_ref, high_ref, low_ref, back_high, back_low = refs[len(layout) : len(layout) + 6]
    outs = refs[len(layout) + 6 : len(layout) + 6 + seq]
    signal, work = refs[len(layout) + 6 + seq :]
    count, rows, width = work.shape
    per = count // seq
    me = me_ref[0]
    for ref, (shift, first) in zip(pieces, layout):
        source = (me - shift + seq) % seq
        for i in range(ref.shape[1] // LANES):
            signal[source * per + first + i] = ref[:, i * LANES : (i + 1) * LANES].astype(F32)
    forward_rows(lambda q, at: signal[q, at, :], twist_ref, work, count)

    def inner(u, carry):
        x = work[pl.ds(u * 4, 4)].reshape(4 * rows, width)
        z = product3(x, high_ref, low_ref)
        h = spec_ref[pl.ds(u * 4, 4)].reshape(4 * rows, width)
        zr, zi = z[:, :LANES], z[:, LANES:]
        hr, hi = h[:, :LANES], h[:, LANES:]
        y = jnp.concatenate([zr * hr - zi * hi, zr * hi + zi * hr], axis=1)
        work[pl.ds(u * 4, 4)] = product3(y, back_high, back_low).reshape(4, rows, width)
        return carry

    lax.fori_loop(0, count // 4, inner, 0)

    def back(r, carry):
        at = pl.ds(pl.multiple_of(r * 8, 8), 8)
        values = []
        for u in range(count):
            c = twist_ref[u : u + 1, :LANES]
            s = twist_ref[u : u + 1, LANES:]
            re = work[u, at, :LANES]
            im = work[u, at, LANES:]
            values.append((re * c - im * s, im * c + re * s))
        for q, (re, im) in enumerate(fft(values, -1)):
            turn = 2 * math.pi * q / (4 * count)
            signal[q, at, :] = re * math.cos(turn) - im * math.sin(turn) if q else re
        return carry

    lax.fori_loop(0, rows // 8, back, 0)
    for shift in range(seq):
        target = (me + shift) % seq
        for i in range(per):
            outs[shift][:, i * LANES : (i + 1) * LANES] = signal[target * per + i].astype(BF16)


def convolve(place, pieces, layout, spec, table, block, index, seq):
    count, channels, width = spec.shape
    twist, high, low, back_high, back_low = table
    const = lambda i, me: (0, 0)
    in_specs = [pl.BlockSpec((block, p.shape[1]), lambda i, me: (index, 0)) for p in pieces]
    in_specs.append(pl.BlockSpec((count, block, width), lambda i, me: (0, index, 0)))
    in_specs += [pl.BlockSpec(a.shape, const) for a in table]
    local = count // seq * LANES
    return pl.pallas_call(
        functools.partial(conv_kernel, layout, seq),
        grid_spec=pltpu.PrefetchScalarGridSpec(
            num_scalar_prefetch=1,
            grid=(1,),
            in_specs=in_specs,
            out_specs=[pl.BlockSpec((block, local), const)] * seq,
            scratch_shapes=[
                pltpu.VMEM((count, block, LANES), F32),
                pltpu.VMEM((count, block, width), F32),
            ],
        ),
        out_shape=[struct((block, local), BF16)] * seq,
        compiler_params=params(dimension_semantics=("arbitrary",)),
        cost_estimate=pl.CostEstimate(
            flops=block * count * 2 * 256 * 256 * 12, transcendentals=0, bytes_accessed=12 * block * count * LANES
        ),
        name="convolve",
    )(place, *pieces, spec, *table)


def gate_kernel(firsts, seq, me_ref, *refs):
    first_refs = refs[:firsts]
    convs = refs[firsts : firsts + seq]
    out_ref, top_ref, low_ref, buffer = refs[-4:]
    me = me_ref[0]
    rows = convs[0].shape[0]
    for shift in range(seq):
        source = (me - shift + seq) % seq
        at = 0
        for f in first_refs:
            width = f.shape[3]
            gate = f[source, 0].astype(F32)
            value = (gate * convs[shift][:, at : at + width].astype(F32)).astype(BF16)
            out_ref[source, 0, :, at : at + width] = value
            buffer[source, :, at : at + width] = value
            at += width
    turned = buffer[...].reshape(seq * rows, buffer.shape[2]).astype(F32).T.astype(BF16)
    half = turned.shape[0] // 2
    top_ref[...] = turned[:half]
    low_ref[...] = turned[half:]


def gate(place, firsts, convs, index, total, previous):
    seq = len(convs)
    rows, time = convs[0].shape
    shape = (seq, total, rows, time)
    in_specs = []
    views = []
    for f in firsts:
        views.append(f.reshape(seq, total, rows, f.shape[1]))
        in_specs.append(
            pl.BlockSpec((seq, 1, rows, f.shape[1]), lambda i, me: (0, index, 0, 0))
        )
    in_specs += [pl.BlockSpec((rows, time), lambda i, me: (0, 0))] * seq
    extra = []
    aliases = {}
    if previous is not None:
        extra = [previous]
        in_specs.append(pl.BlockSpec(memory_space=pl.ANY))
        aliases = {1 + len(firsts) + seq: 0}
    half = struct((time // 2, seq * rows), BF16)
    return pl.pallas_call(
        functools.partial(gate_kernel, len(firsts), seq),
        grid_spec=pltpu.PrefetchScalarGridSpec(
            num_scalar_prefetch=1,
            grid=(1,),
            in_specs=in_specs,
            out_specs=[
                pl.BlockSpec((seq, 1, rows, time), lambda i, me: (0, index, 0, 0)),
                pl.BlockSpec(half.shape, lambda i, me: (0, 0)),
                pl.BlockSpec(half.shape, lambda i, me: (0, 0)),
            ],
            scratch_shapes=[pltpu.VMEM((seq, rows, time), BF16)],
        ),
        out_shape=[struct(shape, BF16), half, half],
        input_output_aliases=aliases,
        compiler_params=params(),
        name="gate",
    )(place, *views, *convs, *extra)


def heads_kernel(slots, previous, me_ref, *refs):
    del me_ref
    tops = refs[:slots]
    lows = refs[slots : 2 * slots]
    weights = refs[2 * slots : 3 * slots]
    out_ref = refs[-1]
    half = tops[0].shape[0]
    for h, parts in enumerate((tops, lows)):
        acc = refs[3 * slots][0, h * half : (h + 1) * half] if previous else None
        for s in range(slots):
            w = weights[s][...].reshape(parts[s].shape[1], weights[s].shape[-1])
            part = jnp.dot(parts[s][...], w, preferred_element_type=F32)
            acc = part if acc is None else acc + part
        out_ref[0, h * half : (h + 1) * half] = acc.astype(out_ref.dtype)


def heads_step(me, tops, lows, weight, index, previous, last):
    slots = len(tops)
    streams, _, seq, total, rows, columns = weight.shape
    half, width = tops[0].shape
    whole = lambda k, me: (0, 0)
    in_specs = [pl.BlockSpec((half, width), whole)] * (2 * slots)
    for s in range(slots):
        in_specs.append(
            pl.BlockSpec(
                (1, 1, seq, 1, rows, columns),
                functools.partial(
                    lambda s, k, me: (k, slot_owner(slots, s, me[0]), 0, index, 0, 0), s
                ),
            )
        )
    extra = []
    aliases = {}
    if previous is not None:
        extra = [previous]
        in_specs.append(pl.BlockSpec((1, 2 * half, columns), lambda k, me: (k, 0, 0)))
        if not last:
            aliases = {1 + 3 * slots: 0}
    return pl.pallas_call(
        functools.partial(heads_kernel, slots, previous is not None),
        grid_spec=pltpu.PrefetchScalarGridSpec(
            num_scalar_prefetch=1,
            grid=(streams,),
            in_specs=in_specs,
            out_specs=pl.BlockSpec((1, 2 * half, columns), lambda k, me: (k, 0, 0)),
        ),
        out_shape=struct((streams, 2 * half, columns), BF16 if last else F32),
        input_output_aliases=aliases,
        compiler_params=params(dimension_semantics=("arbitrary",)),
        cost_estimate=pl.CostEstimate(
            flops=4 * half * width * slots * streams * columns,
            transcendentals=0,
            bytes_accessed=streams * half * columns * 16,
        ),
        name="heads",
    )(me, *tops, *lows, *([weight] * slots), *extra)


def state_kernel(key_ref, value_ref, before_ref, total_ref):
    blocks = before_ref.shape[1]
    running = jnp.zeros((HD, HD), F32)
    for b in range(blocks):
        before_ref[0, b] = running
        span = slice(b * BLOCK, (b + 1) * BLOCK)
        running = running + lax.dot_general(
            key_ref[0, span], value_ref[0, span], (((0,), (0,)), ((), ())), preferred_element_type=F32
        )
    total_ref[0] = running


def block_states(heads):
    _, time, columns = heads.shape
    blocks = time // BLOCK
    count = columns // HD
    spec = lambda k: pl.BlockSpec((1, time, HD), lambda h: (k, 0, h))
    return pl.pallas_call(
        state_kernel,
        grid=(count,),
        in_specs=[spec(1), spec(2)],
        out_specs=[
            pl.BlockSpec((1, blocks, HD, HD), lambda h: (h, 0, 0, 0)),
            pl.BlockSpec((1, HD, HD), lambda h: (h, 0, 0)),
        ],
        out_shape=[struct((count, blocks, HD, HD), F32), struct((count, HD, HD), F32)],
        compiler_params=params(dimension_semantics=("arbitrary",)),
        name="states",
    )(heads, heads)


def inside_kernel(query_ref, key_ref, value_ref, out_ref):
    causal = lax.broadcasted_iota(jnp.int32, (BLOCK, BLOCK), 0) >= lax.broadcasted_iota(
        jnp.int32, (BLOCK, BLOCK), 1
    )
    for b in range(query_ref.shape[1] // BLOCK):
        span = slice(b * BLOCK, (b + 1) * BLOCK)
        scores = lax.dot_general(
            query_ref[0, span], key_ref[0, span], (((1,), (1,)), ((), ())), preferred_element_type=F32
        )
        scores = jnp.where(causal, scores, 0.0).astype(BF16)
        out_ref[span] = jnp.dot(scores, value_ref[0, span], preferred_element_type=F32)


def inside_blocks(heads):
    _, time, columns = heads.shape
    spec = lambda k: pl.BlockSpec((1, time, HD), lambda h: (k, 0, h))
    return pl.pallas_call(
        inside_kernel,
        grid=(columns // HD,),
        in_specs=[spec(0), spec(1), spec(2)],
        out_specs=pl.BlockSpec((time, HD), lambda h: (0, h)),
        out_shape=struct((time, columns), F32),
        compiler_params=params(dimension_semantics=("arbitrary",)),
        cost_estimate=pl.CostEstimate(
            flops=4 * time * BLOCK * columns, transcendentals=0, bytes_accessed=time * columns * 10
        ),
        name="inside",
    )(heads, heads, heads)


def finish_kernel(place_ref, query_ref, inside_ref, before_ref, incoming_ref, out_ref):
    time = query_ref.shape[1]
    first = place_ref[0] * time
    for b in range(time // BLOCK):
        span = slice(b * BLOCK, (b + 1) * BLOCK)
        earlier = (incoming_ref[0] + before_ref[0, b]).astype(BF16)
        carried = jnp.dot(query_ref[0, span], earlier, preferred_element_type=F32)
        position = first + b * BLOCK + 1 + lax.broadcasted_iota(jnp.int32, (BLOCK, HD), 0)
        divisor = jnp.sqrt((position * HD).astype(F32))
        out_ref[span] = ((inside_ref[span] + carried) / divisor).astype(BF16)


def finish(place, heads, inside, before, incoming):
    _, time, columns = heads.shape
    blocks = time // BLOCK
    return pl.pallas_call(
        finish_kernel,
        grid_spec=pltpu.PrefetchScalarGridSpec(
            num_scalar_prefetch=1,
            grid=(columns // HD,),
            in_specs=[
                pl.BlockSpec((1, time, HD), lambda h, me: (0, 0, h)),
                pl.BlockSpec((time, HD), lambda h, me: (0, h)),
                pl.BlockSpec((1, blocks, HD, HD), lambda h, me: (h, 0, 0, 0)),
                pl.BlockSpec((1, HD, HD), lambda h, me: (h, 0, 0)),
            ],
            out_specs=pl.BlockSpec((time, HD), lambda h, me: (0, h)),
        ),
        out_shape=struct((time, columns), BF16),
        compiler_params=params(dimension_semantics=("arbitrary",)),
        name="finish",
    )(place, heads, inside, before, incoming)


def sum_before(part, axis):
    size = lax.axis_size(axis)
    total = None
    run = part
    by = 1
    while by < size:
        received = passed_along(run, axis, by)
        total = received if total is None else total + received
        run = run + received
        by *= 2
    return total


def shards(
    fine_codes,
    coarse_codes,
    frame_order,
    emb_fine,
    emb_coarse,
    norm_gain,
    w_hyena,
    short_taps,
    long_filter,
    w_attn,
):
    time = fine_codes.shape[0]
    seq = lax.axis_size("seq")
    chan = lax.axis_size("chan")
    me = lax.axis_index("chan").astype(jnp.int32).reshape(1)
    place = lax.axis_index("seq").astype(jnp.int32).reshape(1)
    frames = time // FRAME
    channels = w_hyena.shape[2]
    group = channels // short_taps.shape[1]
    weight = jnp.transpose(w_hyena, (1, 0, 2))
    order = frame_order.reshape(1, FRAME)
    fine = fine_codes.reshape(frames, FRAME)
    coarse = coarse_codes.reshape(frames, FRAME // 2)

    last = embed(order, fine[frames - 1 :], coarse[frames - 1 :], emb_fine, emb_coarse, LANES)
    rest = embed(order, fine[: frames - 1], coarse[: frames - 1], emb_fine, emb_coarse, LANES)
    pieces = list(rest) + list(last)
    count = len(pieces)
    gains = gather_piece(norm_gain.reshape(1, -1), "chan", True)
    slots = [None] * count
    for n, i in enumerate([count - 1] + list(range(count - 1))):
        slots[i] = gather_piece(pieces[i], "chan", n % 2 == 0)
    table = tables(seq * time // LANES)
    part = channels // seq
    block = min(64, part)
    spec = spectrum(long_filter, table, block)

    taps = short_taps.astype(F32)
    tail = project(me, [slots[count - 1]], gains, weight)
    rim = passed_along(tail, "seq", 1)
    before = (rim, 0)
    firsts, mixed, layout = [], [], []
    for c in range(count // 2):
        if c < count // 2 - 1:
            out = project(me, slots[2 * c : 2 * c + 2], gains, weight)
            tiles = [before, (out, 0), (out, 1)]
            before = (out, 1)
        else:
            out = project(me, slots[2 * c : 2 * c + 1], gains, weight)
            tiles = [before, (out, 0), (tail, 0)]
        first, mixes = short_filter(place, taps, tiles, seq, group)
        firsts.append(first)
        for shift in range(seq):
            mixed.append(shifted(mixes[shift], "seq", shift) if shift else mixes[0])
            layout.append((shift, 2 * c))

    total = part // block
    attn = jnp.transpose(w_attn, (1, 0, 2)).reshape(3, chan, seq, total, block, w_attn.shape[2])
    hyena = None
    heads = None
    for j in range(total):
        rows = convolve(place, mixed, tuple(layout), spec, table, block, j, seq)
        convs = [shifted(rows[s], "seq", s) if s else rows[0] for s in range(seq)]
        hyena, top, low = gate(place, firsts, convs, j, total, hyena)
        tops = gather_piece(top, "chan", True)
        lows = gather_piece(low, "chan", False)
        heads = heads_step(me, tops, lows, attn, j, heads, j == total - 1)
    hyena_out = hyena.reshape(channels, time)

    before_blocks, device_state = block_states(heads)
    incoming = sum_before(device_state, "seq")
    inside = inside_blocks(heads)
    attn_out = finish(place, heads, inside, before_blocks, incoming)
    return hyena_out, attn_out


def solution(mesh):
    return jax.shard_map(
        shards,
        mesh=mesh,
        in_specs=(
            P(("rep", "seq")),
            P(("rep", "seq")),
            P(),
            P(None, "chan"),
            P(None, "chan"),
            P("chan"),
            P(None, None, "chan"),
            P(None, "chan", None),
            P(("chan", "seq"), None),
            P(None, None, "chan"),
        ),
        out_specs=(P("chan", ("rep", "seq")), P(("rep", "seq"), "chan")),
        check_vma=False,
    )
```

```python
import functools
import math

import jax
import jax.numpy as jnp
import numpy as np
from jax import lax
from jax.experimental import pallas as pl
from jax.experimental.pallas import tpu as pltpu
from jax.sharding import PartitionSpec as P

HD = 128
FRAME = 256
BLOCK = 512
LANES = 128
EPSILON = 1e-05
F32 = jnp.float32
BF16 = jnp.bfloat16
RING = (0, 1, 3, 2)


def params(vmem_mib=20, **kw):
    return pltpu.CompilerParams(vmem_limit_bytes=vmem_mib << 20, **kw)


def struct(shape, dtype):
    return jax.ShapeDtypeStruct(shape, dtype)


def ring_steps():
    forward = [(RING[i], RING[(i + 1) % 4]) for i in range(4)]
    return forward, [(b, a) for a, b in forward]


def gather_piece(piece, axis, clockwise):
    size = lax.axis_size(axis)
    if size == 4:
        forward, backward = ring_steps()
        left = lax.ppermute(piece, axis, forward)
        right = lax.ppermute(piece, axis, backward)
        if clockwise:
            across = lax.ppermute(left, axis, forward)
        else:
            across = lax.ppermute(right, axis, backward)
        return [piece, left, right, across]
    gathered = lax.all_gather(piece, axis)
    return [gathered[i] for i in range(size)]


def slot_owner(size, slot, me):
    if size != 4:
        return slot
    if slot == 0:
        return me
    if slot == 3:
        return 3 - me
    before = jnp.where(me == 0, 2, jnp.where(me == 1, 0, jnp.where(me == 2, 3, 1)))
    return before if slot == 1 else 3 - before


def shifted(piece, axis, by):
    size = lax.axis_size(axis)
    return lax.ppermute(piece, axis, [(i, (i + by) % size) for i in range(size)])


def passed_along(x, axis, by):
    size = lax.axis_size(axis)
    return lax.ppermute(x, axis, [(i, i + by) for i in range(size - by)])


def embed_kernel(order_ref, fine_ref, coarse_ref, fine_table, coarse_table, gain_ref, *outs):
    vocab = fine_table.shape[0]
    order = order_ref[...]
    pick = (order == lax.broadcasted_iota(jnp.int32, (FRAME, FRAME), 0)).astype(F32).T
    half = order >> 1
    pick_half = (half == lax.broadcasted_iota(jnp.int32, (FRAME // 2, FRAME), 0)).astype(F32).T
    codes = lax.broadcasted_iota(jnp.int32, (FRAME, vocab), 1).astype(F32)
    for f, out in enumerate(outs):
        fine = jnp.sum(pick * fine_ref[f : f + 1, :].astype(F32), axis=1, keepdims=True)
        coarse = jnp.sum(pick_half * coarse_ref[f : f + 1, :].astype(F32), axis=1, keepdims=True)
        hot_fine = (codes == fine).astype(F32).astype(BF16)
        hot_coarse = (codes == coarse).astype(F32).astype(BF16)
        total = jnp.dot(hot_fine, fine_table[...], preferred_element_type=F32) + jnp.dot(
            hot_coarse, coarse_table[...], preferred_element_type=F32
        )
        out[:FRAME, :] = total.astype(BF16)
        if out.shape[0] > FRAME:
            extra = (out.shape[0] - FRAME, out.shape[1])
            out[FRAME:, :] = jnp.broadcast_to(gain_ref[...].astype(F32), extra).astype(BF16)


def embed(order, fine, coarse, fine_table, coarse_table, gain, extra):
    width = fine_table.shape[1]
    return pl.pallas_call(
        embed_kernel,
        out_shape=[struct((FRAME + extra, width), BF16)] * fine.shape[0],
        compiler_params=params(),
        name="embed",
    )(order, fine, coarse, fine_table, coarse_table, gain)


def project_kernel(slots, streams, block, me_ref, *refs):
    pieces = refs[:slots]
    gains = refs[slots : 2 * slots]
    weights = refs[2 * slots : 2 * slots + streams]
    outs = refs[2 * slots + streams : -1]
    normed = refs[-1]
    at = pl.program_id(0)
    width = pieces[0].shape[1]

    @pl.when(at == 0)
    def _():
        total = jnp.zeros((FRAME, 1), F32)
        for s in range(slots):
            v = pieces[s][...].astype(F32)
            total = total + jnp.sum(v * v, axis=1, keepdims=True)
        factor = lax.rsqrt(total / (slots * width) + EPSILON)
        for s in range(slots):
            v = pieces[s][...].astype(F32)
            v = v * factor * gains[s][0:1].astype(F32)
            normed[:, s * width : (s + 1) * width] = v.astype(BF16)

    columns = pl.ds(pl.multiple_of(at * block, block), block)
    for k in range(streams):
        acc = None
        for s in range(slots):
            rows = pl.ds(pl.multiple_of(slot_owner(slots, s, me_ref[0]) * width, width), width)
            part = jnp.dot(
                normed[:, s * width : (s + 1) * width],
                weights[k][rows, columns],
                preferred_element_type=F32,
            )
            acc = part if acc is None else acc + part
        turned = acc.T.astype(BF16)
        for n, out in enumerate(outs):
            out[k] = turned[:, n * LANES : (n + 1) * LANES]


def project(me, pieces, gains, weights):
    slots = len(pieces)
    streams = len(weights)
    width = pieces[0].shape[1]
    channels = weights[0].shape[1]
    block = min(512, channels)
    extra = gains[0].shape[0] - FRAME
    count = FRAME // LANES
    in_specs = [pl.BlockSpec((FRAME, width), lambda j, me: (0, 0))] * slots
    in_specs += [pl.BlockSpec((extra, width), lambda j, me: (FRAME // extra, 0))] * slots
    in_specs += [pl.BlockSpec(memory_space=pltpu.VMEM)] * streams
    return pl.pallas_call(
        functools.partial(project_kernel, slots, streams, block),
        grid_spec=pltpu.PrefetchScalarGridSpec(
            num_scalar_prefetch=1,
            grid=(channels // block,),
            in_specs=in_specs,
            out_specs=[pl.BlockSpec((streams, block, LANES), lambda j, me: (0, j, 0))] * count,
            scratch_shapes=[pltpu.VMEM((FRAME, slots * width), BF16)],
        ),
        out_shape=[struct((streams, channels, LANES), BF16)] * count,
        compiler_params=params(12, dimension_semantics=("arbitrary",)),
        cost_estimate=pl.CostEstimate(
            flops=2 * FRAME * streams * channels * slots * width,
            transcendentals=0,
            bytes_accessed=8 * FRAME * slots * width,
        ),
        name="project",
    )(me, *pieces, *gains, *weights)


def short_kernel(pairs, seq, steps, group, me_ref, taps_ref, *refs):
    count = len(pairs)
    tiles = refs[: -1 - seq]
    first_ref = refs[-1 - seq]
    mixes = refs[-seq:]
    step = pl.program_id(0)
    block = tiles[0].shape[1]
    groups = block // group
    part = (step // steps + me_ref[0]) % seq
    base = (part * steps + step % steps) * groups
    row = lax.broadcasted_iota(jnp.int32, (LANES, LANES), 0)
    column = lax.broadcasted_iota(jnp.int32, (LANES, LANES), 1)
    lower = column >= row
    results = []
    for g in range(groups):
        span = slice(g * group, (g + 1) * group)
        outs = []
        for k in range(3):
            tap = jnp.broadcast_to(taps_ref[k, pl.ds(base + g, 1), :], (LANES, LANES))
            turned = pltpu.roll(tap, 0, 1, stride=1, stride_axis=0)
            matrix = jnp.concatenate(
                [jnp.where(lower, 0.0, turned), jnp.where(lower, turned, 0.0)], axis=0
            ).astype(BF16)
            data = [t[k, span, :] for t in tiles]
            window = jnp.concatenate(
                [jnp.concatenate([data[a], data[b]], axis=1) for a, b in pairs], axis=0
            )
            outs.append(jnp.dot(window, matrix, preferred_element_type=F32).astype(BF16))
        mix = (outs[1].astype(F32) * outs[2].astype(F32)).astype(BF16)
        results.append((span, outs[0], mix))
    for span, first, mix in results:
        for n in range(count):
            first_ref[span, n * LANES : (n + 1) * LANES] = first[n * group : (n + 1) * group]
    for s in range(seq):

        @pl.when(step // steps == s)
        def _():
            for span, first, mix in results:
                for n in range(count):
                    mixes[s][span, n * LANES : (n + 1) * LANES] = mix[n * group : (n + 1) * group]


def short_filter(place, taps, tiles, pairs, seq, group):
    count = len(pairs)
    streams, channels, _ = tiles[0].shape
    part = channels // seq
    block = min(LANES, part)
    steps = part // block

    def natural(i, me):
        return ((i // steps + me[0]) % seq) * steps + i % steps

    in_specs = [pl.BlockSpec(taps.shape, lambda i, me: (0, 0, 0))]
    in_specs += [pl.BlockSpec((streams, block, LANES), lambda i, me: (0, natural(i, me), 0))] * len(tiles)
    out_specs = [pl.BlockSpec((block, count * LANES), lambda i, me: (natural(i, me), 0))]
    for s in range(seq):
        out_specs.append(
            pl.BlockSpec(
                (block, count * LANES),
                functools.partial(
                    lambda s, i, me: (jnp.clip(i - s * steps, 0, steps - 1), 0), s
                ),
            )
        )
    outs = pl.pallas_call(
        functools.partial(short_kernel, tuple(pairs), seq, steps, group),
        grid_spec=pltpu.PrefetchScalarGridSpec(
            num_scalar_prefetch=1, grid=(seq * steps,), in_specs=in_specs, out_specs=out_specs
        ),
        out_shape=[struct((channels, count * LANES), BF16)]
        + [struct((part, count * LANES), BF16)] * seq,
        compiler_params=params(8, dimension_semantics=("arbitrary",)),
        cost_estimate=pl.CostEstimate(
            flops=2 * streams * channels * count * LANES * 2 * LANES * 4,
            transcendentals=0,
            bytes_accessed=2 * channels * LANES * (4 * streams + 4 * count),
        ),
        name="short_filter",
    )(place, taps, *tiles)
    return outs[0], outs[1:]


def times_root(value, turn):
    re, im = value
    eighths = turn * 8 % 8
    if eighths == 0:
        return re, im
    if eighths == 2:
        return im, -re
    if eighths == 4:
        return -re, -im
    if eighths == 6:
        return -im, re
    if eighths in (1, 3, 5, 7):
        h = math.sqrt(0.5)
        c = h if eighths in (1, 7) else -h
        s = h if eighths in (1, 3) else -h
        if c == s:
            return (re + im) * c, (im - re) * c
        return (re - im) * c, (im + re) * c
    c, s = math.cos(2 * math.pi * turn), math.sin(2 * math.pi * turn)
    return re * c + im * s, im * c - re * s


def fft(values, sign):
    n = len(values)
    if n == 1:
        return values
    even = fft(values[0::2], sign)
    odd = fft(values[1::2], sign)
    low, high = [], []
    for k in range(n // 2):
        er, ei = even[k]
        tr, ti = times_root(odd[k], sign * k / n)
        low.append((er + tr, ei + ti))
        high.append((er - tr, ei - ti))
    return low + high


def split(x):
    high = x.astype(BF16)
    return high, (x - high.astype(F32)).astype(BF16)


def product3(x, high_ref, low_ref):
    high, low = split(x)
    return (
        jnp.dot(high, low_ref[...], preferred_element_type=F32)
        + jnp.dot(low, high_ref[...], preferred_element_type=F32)
        + jnp.dot(high, high_ref[...], preferred_element_type=F32)
    )


def forward_rows(load, twist_ref, work, count):
    def body(r, carry):
        at = pl.ds(pl.multiple_of(r * 8, 8), 8)
        values = []
        for q in range(count):
            x = load(q, at)
            turn = 2 * math.pi * q / (4 * count)
            values.append((x * math.cos(turn), x * -math.sin(turn)) if q else (x, jnp.zeros_like(x)))
        for u, (re, im) in enumerate(fft(values, 1)):
            c = twist_ref[u : u + 1, :LANES]
            s = twist_ref[u : u + 1, LANES:]
            work[u, at, :LANES] = re * c + im * s
            work[u, at, LANES:] = im * c - re * s
        return carry

    lax.fori_loop(0, work.shape[1] // 8, body, 0)


def spectrum_kernel(x_ref, twist_ref, high_ref, low_ref, weight_ref, *refs):
    work, sem = refs[-2:]
    streams = weight_ref.shape[0]
    held = refs[-2 - streams : -2]
    out_ref = refs[-3 - streams]
    count, rows, width = work.shape
    copies = [pltpu.make_async_copy(weight_ref.at[k], held[k], sem.at[k]) for k in range(streams)]

    @pl.when(pl.program_id(0) == 0)
    def _():
        for copy in copies:
            copy.start()

    forward_rows(lambda q, at: x_ref[at, q * LANES : (q + 1) * LANES], twist_ref, work, count)
    scale = 2.0 / (2 * count * LANES)

    def inner(u, carry):
        x = work[pl.ds(u * 4, 4)].reshape(4 * rows, width)
        out_ref[pl.ds(u * 4, 4)] = (product3(x, high_ref, low_ref) * scale).reshape(4, rows, width)
        return carry

    lax.fori_loop(0, count // 4, inner, 0)

    @pl.when(pl.program_id(0) == pl.num_programs(0) - 1)
    def _():
        for copy in copies:
            copy.wait()


def tables(count):
    total = 2 * count * LANES
    u = np.arange(count)[:, None]
    k = np.arange(LANES)[None, :]
    angle = 2 * np.pi * (2 * u + 0.5) * k / total
    twist = np.concatenate([np.cos(angle), np.sin(angle)], axis=1).astype(np.float32)
    inner = 2 * np.pi * (np.arange(LANES)[:, None] * k % LANES) / LANES
    c, s = np.cos(inner), np.sin(inner)
    matrix = np.block([[c, -s], [s, c]]).astype(np.float32)
    high = matrix.astype(jnp.bfloat16)
    low = (matrix - high.astype(np.float32)).astype(jnp.bfloat16)
    return (
        jnp.asarray(twist),
        jnp.asarray(high),
        jnp.asarray(low),
        jnp.asarray(high.T.copy()),
        jnp.asarray(low.T.copy()),
    )


def spectrum(response, table, block, weight, early):
    channels, length = response.shape
    count = length // LANES
    twist, high, low = table[:3]
    const = lambda i: (0, 0)
    return pl.pallas_call(
        spectrum_kernel,
        grid=(channels // block,),
        in_specs=[
            pl.BlockSpec((block, length), lambda i: (i, 0)),
            pl.BlockSpec(twist.shape, const),
            pl.BlockSpec(high.shape, const),
            pl.BlockSpec(low.shape, const),
        ]
        + [pl.BlockSpec(memory_space=pl.ANY)] * (1 + len(early)),
        out_specs=[
            pl.BlockSpec((count, block, 2 * LANES), lambda i: (0, i, 0)),
        ]
        + [pl.BlockSpec(memory_space=pltpu.VMEM)] * weight.shape[0],
        out_shape=[
            pltpu.HBM((count, channels, 2 * LANES), F32),
        ]
        + [pltpu.VMEM(weight.shape[1:], weight.dtype)] * weight.shape[0],
        scratch_shapes=[
            pltpu.VMEM((count, block, 2 * LANES), F32),
            pltpu.SemaphoreType.DMA((weight.shape[0],)),
        ],
        compiler_params=params(12, dimension_semantics=("arbitrary",)),
        cost_estimate=pl.CostEstimate(
            flops=channels * count * 2 * 256 * 256 * 6, transcendentals=0, bytes_accessed=12 * channels * length
        ),
        name="spectrum",
    )(response, twist, high, low, pltpu.with_memory_space_constraint(weight, pltpu.HBM), *early)


def conv_kernel(layout, seq, me_ref, *refs):
    pieces = refs[: len(layout)]
    spec_ref, twist_ref, high_ref, low_ref, back_high, back_low = refs[len(layout) : len(layout) + 6]
    outs = refs[len(layout) + 6 : len(layout) + 6 + seq]
    signal, work = refs[len(layout) + 6 + seq :]
    count, rows, width = work.shape
    per = count // seq
    me = me_ref[0]
    for ref, (shift, spots) in zip(pieces, layout):
        source = (me - shift + seq) % seq
        for i, spot in enumerate(spots):
            signal[source * per + spot] = ref[:, i * LANES : (i + 1) * LANES].astype(F32)
    forward_rows(lambda q, at: signal[q, at, :], twist_ref, work, count)

    def inner(u, carry):
        x = work[pl.ds(u * 4, 4)].reshape(4 * rows, width)
        z = product3(x, high_ref, low_ref)
        h = spec_ref[pl.ds(u * 4, 4)].reshape(4 * rows, width)
        zr, zi = z[:, :LANES], z[:, LANES:]
        hr, hi = h[:, :LANES], h[:, LANES:]
        y = jnp.concatenate([zr * hr - zi * hi, zr * hi + zi * hr], axis=1)
        work[pl.ds(u * 4, 4)] = product3(y, back_high, back_low).reshape(4, rows, width)
        return carry

    lax.fori_loop(0, count // 4, inner, 0)

    def back(r, carry):
        at = pl.ds(pl.multiple_of(r * 8, 8), 8)
        values = []
        for u in range(count):
            c = twist_ref[u : u + 1, :LANES]
            s = twist_ref[u : u + 1, LANES:]
            re = work[u, at, :LANES]
            im = work[u, at, LANES:]
            values.append((re * c - im * s, im * c + re * s))
        for q, (re, im) in enumerate(fft(values, -1)):
            turn = 2 * math.pi * q / (4 * count)
            signal[q, at, :] = re * math.cos(turn) - im * math.sin(turn) if q else re
        return carry

    lax.fori_loop(0, rows // 8, back, 0)
    for shift in range(seq):
        target = (me + shift) % seq
        for i in range(per):
            outs[shift][:, i * LANES : (i + 1) * LANES] = signal[target * per + i].astype(BF16)


def convolve(place, pieces, layout, spec, table, block, start, seq):
    count, _, width = spec.shape
    index = start // block
    const = lambda i, me: (0, 0)
    in_specs = [pl.BlockSpec((block, p.shape[1]), lambda i, me: (index, 0)) for p in pieces]
    spec = pltpu.with_memory_space_constraint(spec, pltpu.HBM)
    in_specs.append(pl.BlockSpec((count, block, width), lambda i, me: (0, index, 0)))
    in_specs += [pl.BlockSpec(a.shape, const) for a in table]
    local = count // seq * LANES
    return pl.pallas_call(
        functools.partial(conv_kernel, layout, seq),
        grid_spec=pltpu.PrefetchScalarGridSpec(
            num_scalar_prefetch=1,
            grid=(1,),
            in_specs=in_specs,
            out_specs=[pl.BlockSpec((block, local), const)] * seq,
            scratch_shapes=[
                pltpu.VMEM((count, block, LANES), F32),
                pltpu.VMEM((count, block, width), F32),
            ],
        ),
        out_shape=[struct((block, local), BF16)] * seq,
        compiler_params=params(dimension_semantics=("arbitrary",)),
        cost_estimate=pl.CostEstimate(
            flops=block * count * 2 * 256 * 256 * 12, transcendentals=0, bytes_accessed=12 * block * count * LANES
        ),
        name="convolve",
    )(place, *pieces, spec, *table)


def gate_kernel(spots, seq, me_ref, *refs):
    first_refs = refs[: len(spots)]
    convs = refs[len(spots) : len(spots) + seq]
    outs = refs[len(spots) + seq :]
    buffer = outs[-1]
    out_ref = [r for r in outs if len(r.shape) == 4][-1]
    turns = [r for r in outs if len(r.shape) == 2]
    me = me_ref[0]
    rows = convs[0].shape[0]
    for shift in range(seq):
        source = (me - shift + seq) % seq
        for f, tiles in zip(first_refs, spots):
            for i, tile in enumerate(tiles):
                at = slice(tile * LANES, (tile + 1) * LANES)
                first = f[source, 0, :, i * LANES : (i + 1) * LANES].astype(F32)
                value = (first * convs[shift][:, at].astype(F32)).astype(BF16)
                out_ref[source, 0, :, at] = value
                buffer[source, :, at] = value
    turned = buffer[...].reshape(seq * rows, buffer.shape[2]).astype(F32).T.astype(BF16)
    share = turned.shape[0] // len(turns)
    for i, turn in enumerate(turns):
        turn[...] = turned[i * share : (i + 1) * share]


def gate(place, firsts, spots, convs, start, part, cuts, previous):
    seq = len(convs)
    rows, time = convs[0].shape
    total = part // rows
    index = start // rows
    shape = (seq, total, rows, time)
    in_specs = []
    views = []
    for f in firsts:
        views.append(f.reshape(seq, total, rows, f.shape[1]))
        in_specs.append(
            pl.BlockSpec((seq, 1, rows, f.shape[1]), lambda i, me: (0, index, 0, 0))
        )
    in_specs += [pl.BlockSpec((rows, time), lambda i, me: (0, 0))] * seq
    extra = []
    aliases = {}
    if previous is not None:
        extra = [previous.reshape(shape)]
        in_specs.append(pl.BlockSpec(memory_space=pl.ANY))
        aliases = {1 + len(firsts) + seq: 0}
    turn = struct((time // cuts, seq * rows), BF16)
    return pl.pallas_call(
        functools.partial(gate_kernel, tuple(spots), seq),
        grid_spec=pltpu.PrefetchScalarGridSpec(
            num_scalar_prefetch=1,
            grid=(1,),
            in_specs=in_specs,
            out_specs=[pl.BlockSpec((seq, 1, rows, time), lambda i, me: (0, index, 0, 0))]
            + [pl.BlockSpec(turn.shape, lambda i, me: (0, 0))] * cuts,
            scratch_shapes=[pltpu.VMEM((seq, rows, time), BF16)],
        ),
        out_shape=[struct(shape, BF16)] + [turn] * cuts,
        input_output_aliases=aliases,
        compiler_params=params(),
        name="gate",
    )(place, *views, *convs, *extra)


def heads_kernel(slots, cuts, previous, me_ref, *refs):
    del me_ref
    weights = refs[slots * cuts : slots * (cuts + 1)]
    out_ref = refs[-1]
    share = refs[0].shape[0]
    for h in range(cuts):
        span = slice(h * share, (h + 1) * share)
        acc = refs[slots * (cuts + 1)][0, span] if previous else None
        for s in range(slots):
            data = refs[h * slots + s]
            w = weights[s][...].reshape(data.shape[1], weights[s].shape[-1])
            part = jnp.dot(data[...], w, preferred_element_type=F32)
            acc = part if acc is None else acc + part
        out_ref[0, span] = acc.astype(out_ref.dtype)


def heads_step(me, groups, weight, first, streams, index, previous, last):
    cuts = len(groups)
    slots = len(groups[0])
    _, _, seq, _, rows, columns = weight.shape
    share, width = groups[0][0].shape
    time = cuts * share
    in_specs = [pl.BlockSpec((share, width), lambda k, me: (0, 0))] * (cuts * slots)
    for s in range(slots):
        in_specs.append(
            pl.BlockSpec(
                (1, 1, seq, 1, rows, columns),
                functools.partial(
                    lambda s, k, me: (first + k, slot_owner(slots, s, me[0]), 0, index, 0, 0), s
                ),
            )
        )
    extra = []
    aliases = {}
    if previous is not None:
        extra = [previous]
        in_specs.append(pl.BlockSpec((1, time, columns), lambda k, me: (k, 0, 0)))
        if not last:
            aliases = {1 + slots * (cuts + 1): 0}
    return pl.pallas_call(
        functools.partial(heads_kernel, slots, cuts, previous is not None),
        grid_spec=pltpu.PrefetchScalarGridSpec(
            num_scalar_prefetch=1,
            grid=(streams,),
            in_specs=in_specs,
            out_specs=pl.BlockSpec((1, time, columns), lambda k, me: (k, 0, 0)),
        ),
        out_shape=struct((streams, time, columns), BF16 if last else F32),
        input_output_aliases=aliases,
        compiler_params=params(40, dimension_semantics=("arbitrary",)),
        cost_estimate=pl.CostEstimate(
            flops=2 * time * width * slots * streams * columns,
            transcendentals=0,
            bytes_accessed=streams * time * columns * 8,
        ),
        name="heads",
    )(me, *[x for g in groups for x in g], *([weight] * slots), *extra)


def state_kernel(key_ref, value_ref, before_ref, total_ref):
    blocks = before_ref.shape[1]
    running = jnp.zeros((HD, HD), F32)
    for b in range(blocks):
        before_ref[0, b] = running
        span = slice(b * BLOCK, (b + 1) * BLOCK)
        running = running + lax.dot_general(
            key_ref[0, span], value_ref[0, span], (((0,), (0,)), ((), ())), preferred_element_type=F32
        )
    total_ref[0] = running


def block_states(pair):
    _, time, columns = pair.shape
    blocks = time // BLOCK
    count = columns // HD
    spec = lambda k: pl.BlockSpec((1, time, HD), lambda h: (k, 0, h))
    return pl.pallas_call(
        state_kernel,
        grid=(count,),
        in_specs=[spec(0), spec(1)],
        out_specs=[
            pl.BlockSpec((1, blocks, HD, HD), lambda h: (h, 0, 0, 0)),
            pl.BlockSpec((1, HD, HD), lambda h: (h, 0, 0)),
        ],
        out_shape=[struct((count, blocks, HD, HD), F32), struct((count, HD, HD), F32)],
        compiler_params=params(dimension_semantics=("arbitrary",)),
        name="states",
    )(pair, pair)


def inside_kernel(query_ref, key_ref, value_ref, out_ref):
    causal = lax.broadcasted_iota(jnp.int32, (BLOCK, BLOCK), 0) >= lax.broadcasted_iota(
        jnp.int32, (BLOCK, BLOCK), 1
    )
    for b in range(query_ref.shape[1] // BLOCK):
        span = slice(b * BLOCK, (b + 1) * BLOCK)
        scores = lax.dot_general(
            query_ref[0, span], key_ref[0, span], (((1,), (1,)), ((), ())), preferred_element_type=F32
        )
        scores = jnp.where(causal, scores, 0.0).astype(BF16)
        out_ref[span] = jnp.dot(scores, value_ref[0, span], preferred_element_type=F32)


def inside_blocks(query, pair):
    _, time, columns = query.shape
    spec = lambda k: pl.BlockSpec((1, time, HD), lambda h: (k, 0, h))
    return pl.pallas_call(
        inside_kernel,
        grid=(columns // HD,),
        in_specs=[spec(0), spec(0), spec(1)],
        out_specs=pl.BlockSpec((time, HD), lambda h: (0, h)),
        out_shape=struct((time, columns), F32),
        compiler_params=params(dimension_semantics=("arbitrary",)),
        cost_estimate=pl.CostEstimate(
            flops=4 * time * BLOCK * columns, transcendentals=0, bytes_accessed=time * columns * 10
        ),
        name="inside",
    )(query, pair, pair)


def finish_kernel(place_ref, query_ref, inside_ref, before_ref, incoming_ref, out_ref):
    time = query_ref.shape[1]
    first = place_ref[0] * time
    for b in range(time // BLOCK):
        span = slice(b * BLOCK, (b + 1) * BLOCK)
        earlier = (incoming_ref[0] + before_ref[0, b]).astype(BF16)
        carried = jnp.dot(query_ref[0, span], earlier, preferred_element_type=F32)
        position = first + b * BLOCK + 1 + lax.broadcasted_iota(jnp.int32, (BLOCK, HD), 0)
        divisor = jnp.sqrt((position * HD).astype(F32))
        out_ref[span] = ((inside_ref[span] + carried) / divisor).astype(BF16)


def finish(place, query, inside, before, incoming):
    _, time, columns = query.shape
    blocks = time // BLOCK
    return pl.pallas_call(
        finish_kernel,
        grid_spec=pltpu.PrefetchScalarGridSpec(
            num_scalar_prefetch=1,
            grid=(columns // HD,),
            in_specs=[
                pl.BlockSpec((1, time, HD), lambda h, me: (0, 0, h)),
                pl.BlockSpec((time, HD), lambda h, me: (0, h)),
                pl.BlockSpec((1, blocks, HD, HD), lambda h, me: (h, 0, 0, 0)),
                pl.BlockSpec((1, HD, HD), lambda h, me: (h, 0, 0)),
            ],
            out_specs=pl.BlockSpec((time, HD), lambda h, me: (0, h)),
        ),
        out_shape=struct((time, columns), BF16),
        compiler_params=params(dimension_semantics=("arbitrary",)),
        name="finish",
    )(place, query, inside, before, incoming)


def sum_before(part, axis):
    size = lax.axis_size(axis)
    total = None
    run = part
    by = 1
    while by < size:
        received = passed_along(run, axis, by)
        total = received if total is None else total + received
        run = run + received
        by *= 2
    return total


def shards(
    fine_codes,
    coarse_codes,
    frame_order,
    emb_fine,
    emb_coarse,
    norm_gain,
    w_hyena,
    short_taps,
    long_filter,
    w_attn,
):
    time = fine_codes.shape[0]
    seq = lax.axis_size("seq")
    chan = lax.axis_size("chan")
    me = lax.axis_index("chan").astype(jnp.int32).reshape(1)
    place = lax.axis_index("seq").astype(jnp.int32).reshape(1)
    frames = time // FRAME
    channels = w_hyena.shape[2]
    group = channels // short_taps.shape[1]
    weight = jnp.transpose(w_hyena, (1, 0, 2))
    order = frame_order.reshape(1, FRAME)
    fine = fine_codes.reshape(frames, FRAME)
    coarse = coarse_codes.reshape(frames, FRAME // 2)

    gain = norm_gain.reshape(1, -1)

    final = frames - 1
    sent = embed(order, fine[final:], coarse[final:], emb_fine, emb_coarse, gain, 16)
    sent += embed(order, fine[:final], coarse[:final], emb_fine, emb_coarse, gain, 0)
    slots = []
    for n, piece in enumerate(sent):
        if slots and chan == 4:
            held = slots[-1][1]
            piece, slots[-1][1] = lax.optimization_barrier((piece, held))
        slots.append(gather_piece(piece, "chan", n % 2 == 0))
    gains = slots[0]
    table = tables(seq * time // LANES)
    part = channels // seq
    taps = short_taps.astype(F32)
    spec, *weights = spectrum(long_filter, table, min(64, part), weight, (me, place, taps))

    tail = project(me, slots[0], gains, weights)
    rim = passed_along(tail[1], "seq", 1)
    before = rim
    firsts, spots, mixed, layout = [], [], [], []
    for f in range(final):
        tiles = [before] + list(project(me, slots[f + 1], gains, weights))
        before = tiles[2]
        pairs = [(0, 1), (1, 2)]
        spot = [2 * f, 2 * f + 1]
        if f == 0:
            pairs.append((3, 4))
            tiles += tail
            spot.append(2 * final + 1)
        if f == final - 1:
            pairs.append((2, len(tiles)))
            tiles.append(tail[0])
            spot.append(2 * final)
        first, mixes = short_filter(place, taps, tiles, pairs, seq, group)
        firsts.append(first)
        spots.append(tuple(spot))
        for shift in range(seq):
            mixed.append(shifted(mixes[shift], "seq", shift) if shift else mixes[0])
            layout.append((shift, tuple(spot)))

    attn = jnp.transpose(w_attn, (1, 0, 2))
    if part % 256 == 0:
        blocks = [(0, part // 4, 1), (part // 4, part // 4, 1), (part // 2, part // 2, 2)]
    else:
        blocks = [(0, part, 1)]
    hyena = query = pair = None
    for n, (start, size, cuts) in enumerate(blocks):
        rows = convolve(place, mixed, tuple(layout), spec, table, size, start, seq)
        convs = [shifted(rows[s], "seq", s) if s else rows[0] for s in range(seq)]
        hyena, *turned = gate(place, firsts, spots, convs, start, part, cuts, hyena)
        groups = [gather_piece(t, "chan", (n + i) % 2 == 0) for i, t in enumerate(turned)]
        view = attn.reshape(3, chan, seq, part // size, size, attn.shape[2])
        last = n == len(blocks) - 1
        pair = heads_step(me, groups, view, 1, 2, start // size, pair, last)
        if last:
            before_blocks, device_state = block_states(pair)
        query = heads_step(me, groups, view, 0, 1, start // size, query, last)
    hyena_out = hyena.reshape(channels, time)

    incoming = sum_before(device_state, "seq")
    inside = inside_blocks(query, pair)
    attn_out = finish(place, query, inside, before_blocks, incoming)
    return hyena_out, attn_out


def solution(mesh):
    return jax.shard_map(
        shards,
        mesh=mesh,
        in_specs=(
            P(("rep", "seq")),
            P(("rep", "seq")),
            P(),
            P(None, "chan"),
            P(None, "chan"),
            P("chan"),
            P(None, None, "chan"),
            P(None, "chan", None),
            P(("chan", "seq"), None),
            P(None, None, "chan"),
        ),
        out_specs=(P("chan", ("rep", "seq")), P(("rep", "seq"), "chan")),
        check_vma=False,
    )
```
